128 devices in a mesh: prow: 8 (over y_lo, z), pcol: 16 (over x, y_hi, core).
Axes of the slice: x: 4, y: 4 (y_hi: 2, y_lo: 2; y = y_hi * 2 + y_lo), z: 4, core: 2. Of those that a mesh axis runs over, the one named last changes fastest.
Arguments:
- anc_inverse: float32 [4096, 4096], P('pcol', 'prow')
- pattern_one: int32 [16, 8], replicated, may hold values from 0 to 15, as said below
- parents: int32 [16], replicated, may hold values from 0 to 15, as said below
- low_one: float32 [16, 2048, 256], P('pcol', 'prow'), may hold values from -2 to 2
- pivot_one: float32 [16, 256, 256], P('pcol'), may hold values from -4 to 4
- low_two: float32 [16, 2048, 256], P('pcol', 'prow'), may hold values from -2 to 2
- second_scaled_factor: float32 [16, 256, 256], P('pcol'), may hold values from -2 to 2
- second_pivot_inverse: float32 [16, 256, 256], P('pcol'), may hold values from -4 to 4
Outputs:
- column_one: float32 [16, 4096, 256], P('prow', 'pcol')
- diag_one: float32 [16, 256, 256], P('pcol')
- column_two: float32 [16, 4096, 256], P('prow', 'pcol')
- second_parent_inverse: float32 [16, 256, 256], P('pcol')
- second_diagonal_inverse: float32 [16, 256, 256], P('pcol')
The draws below stay inside these ranges and needn't reach their ends.
Inputs may be any that keep to these rules, and one draw needn't show every extreme that they name: `pattern_one`: entry r of each row names an ancestor of process row r: it lies in r * 2 to r * 2 + 1; for each r, every ancestor of that range is entry r of exactly 8 rows. `parents`: every first-level supernode is the parent of exactly one second-level supernode.
All inputs are finite; a program needn't handle non-finite values.
Results may differ from the reference program's by a relative error of at most 0.000073.
Values sent between devices are 32-bit elements; how exact they have to be, the bound alone decides.
No kernel may reach another device: no remote copies, remote signals or barrier semaphores. Data moves between devices by JAX's collectives and lax.ppermute only.
A program may use at most 128 MiB of HBM per device.

```python
import jax
import jax.numpy as jnp
from jax import lax

B = 256
NA = 16
P_SIZE = 8
CB = 2
K1 = 16
M2 = 16


def draw_anc_inverse(key, part):
    total = NA * B
    noise = jax.random.normal(key, (total, total), jnp.float32)
    symmetric = (noise + noise.T) * (0.35 / jnp.sqrt(2.0 * total))
    return jnp.eye(total, dtype=jnp.float32) + symmetric


def draw_pattern_one(key, part):
    column_keys = jax.random.split(jax.random.fold_in(key, 17), P_SIZE)
    base = (jnp.arange(K1, dtype=jnp.int32) % CB).astype(jnp.int32)
    offsets = jax.vmap(lambda k: jax.random.permutation(k, base))(column_keys).T
    starts = jnp.arange(P_SIZE, dtype=jnp.int32)[None, :] * CB
    return (offsets + starts).astype(jnp.int32)


def draw_parents(key, part):
    base = (jnp.arange(M2, dtype=jnp.int32) % K1).astype(jnp.int32)
    return jax.random.permutation(jax.random.fold_in(key, 29), base).astype(jnp.int32)


def block_levels(rng, shape, cuts, least, high):
    def one(position, shards_of):
        heights = jax.random.uniform(jax.random.fold_in(jax.random.fold_in(rng, 6), position), (shards_of,), jnp.float32, least / len(cuts), high / len(cuts))
        return jnp.repeat(jnp.exp(heights), shape[position] // shards_of).reshape((-1,) + (1,) * (len(shape) - position - 1))

    gain = one(*cuts[0])
    for cut in cuts[1:]:
        gain = gain * one(*cut)
    return gain


def gaussian(key, dims, scale, limit, cuts=(), kind=jnp.bfloat16):
    result = scale * jax.random.normal(key, dims, jnp.float32)
    if cuts:
        result = result * block_levels(key, dims, cuts, -0.22, 0.18)
    return jnp.clip(result, -limit, limit).astype(kind)


def setup_inputs(seed: int = 0) -> dict:
    splits = jax.random.split(jax.random.key(seed), 9)
    anc_inverse = draw_anc_inverse(jax.random.fold_in(splits[8], 71), 0)
    pattern_one = draw_pattern_one(jax.random.fold_in(splits[8], 71), 0)
    parents = draw_parents(jax.random.fold_in(splits[8], 71), 0)
    low_one = gaussian(splits[3], (K1, P_SIZE * B, B), 0.15, 2.0, ((0, 16), (1, 8)), jnp.float32)
    pivot_one = gaussian(splits[4], (K1, B, B), 0.3, 4.0, ((0, 16),), jnp.float32)
    low_two = gaussian(splits[5], (M2, P_SIZE * B, B), 0.15, 2.0, ((0, 16), (1, 8)), jnp.float32)
    second_scaled_factor = gaussian(splits[6], (M2, B, B), 0.15, 2.0, ((0, 16),), jnp.float32)
    second_pivot_inverse = gaussian(splits[7], (M2, B, B), 0.3, 4.0, ((0, 16),), jnp.float32)
    return {"anc_inverse": anc_inverse, "pattern_one": pattern_one, "parents": parents, "low_one": low_one, "pivot_one": pivot_one, "low_two": low_two, "second_scaled_factor": second_scaled_factor, "second_pivot_inverse": second_pivot_inverse}


def reference(anc_inverse, pattern_one, parents, low_one, pivot_one, low_two, second_scaled_factor, second_pivot_inverse):
    highest_accuracy = lax.Precision.HIGHEST
    blocks = anc_inverse.reshape(NA, B, NA, B).transpose(0, 2, 1, 3)
    lower_one = low_one.reshape(K1, P_SIZE, B, B)
    lower_two = low_two.reshape(M2, P_SIZE, B, B)

    def first_column(args):
        slots, factor = args
        chosen = blocks[:, slots]
        return -jnp.einsum('iprs,pst->irt', chosen, factor, precision=highest_accuracy)

    column_full = lax.map(first_column, (pattern_one, lower_one))
    on_slots = jax.vmap(lambda z, s: z[s])(column_full, pattern_one)
    diag_one = pivot_one - jnp.einsum('kpsa,kpsb->kab', lower_one, on_slots, precision=highest_accuracy)

    pattern_two = pattern_one[parents]
    parent_column = column_full[parents]

    def second_column(args):
        slots, factor, upper, parent_block = args
        chosen = blocks[:, slots]
        local_sum = jnp.einsum('iprs,pst->irt', chosen, factor, precision=highest_accuracy)
        carried = jnp.einsum('irs,st->irt', parent_block, upper, precision=highest_accuracy)
        return -(carried + local_sum)

    column_two_full = lax.map(second_column, (pattern_two, lower_two, second_scaled_factor, parent_column))
    parent_slots = on_slots[parents]
    second_parent_inverse = -(jnp.einsum('mab,mbd->mad', diag_one[parents], second_scaled_factor, precision=highest_accuracy)
                  + jnp.einsum('mpsa,mpsb->mab', parent_slots, lower_two, precision=highest_accuracy))
    second_on_slots = jax.vmap(lambda z, s: z[s])(column_two_full, pattern_two)
    second_diagonal_inverse = (second_pivot_inverse - jnp.einsum('oik,oiu->oku', second_scaled_factor, second_parent_inverse, precision=highest_accuracy)
                - jnp.einsum('mpsa,mpsb->mab', lower_two, second_on_slots, precision=highest_accuracy))
    column_one = column_full.reshape(K1, NA * B, B)
    column_two = column_two_full.reshape(M2, NA * B, B)
    return (column_one, diag_one, column_two, second_parent_inverse, second_diagonal_inverse)
```

```python
import functools

import jax
import jax.numpy as jnp
from jax import lax
from jax.experimental import pallas as pl
from jax.experimental.pallas import tpu as pltpu
from jax.sharding import Mesh, PartitionSpec as P

ROWS, CHIPS, CORES = "prow", "chip", "core"


def split(x):
    high = x.astype(jnp.bfloat16)
    return high, (x - high.astype(jnp.float32)).astype(jnp.bfloat16)


def product(a, b, a_dim=1, b_dim=0):
    dims = (((a_dim,), (b_dim,)), ((), ()))
    dot = functools.partial(lax.dot_general, dimension_numbers=dims, preferred_element_type=jnp.float32)
    (ah, al), (bh, bl) = split(a), split(b)
    return dot(ah, bh) + (dot(ah, bl) + dot(al, bh))


def kernel(info, own, other, low, low_here, factor, pivot, keep, give, parts, total):
    r = pl.program_id(0)
    width = own.shape[-1]

    @pl.when(r == 0)
    def _():
        total[...] = jnp.zeros_like(total)

    def blocks(ref):
        piece = ref.shape[1] // 2
        one = ref[:, :piece, :].reshape(width, width)
        return one, ref[:, piece:, :].reshape(width, width)

    left = jnp.concatenate([own[0], other[0]], axis=0)
    right = jnp.concatenate(blocks(low), axis=1)
    total[...] += product(left, right)

    @pl.when(r == pl.num_programs(0) - 1)
    def _():
        upper = factor[...].reshape(width, width)
        one = total[:, :width]
        two = product(one, upper) - total[:, width:]
        keep[0] = -one[:width]
        give[0] = -one[width:]
        keep[1] = two[:width]
        give[1] = two[width:]
        second = info[8] > 0
        slot_one = jnp.where(second, give[0], keep[0])
        slot_two = jnp.where(second, give[1], keep[1])
        low_one, low_two = blocks(low_here)
        here = jnp.where(info[9] > 0, pivot[0], jnp.zeros_like(slot_one))
        diag = here - product(low_one, slot_one, 0, 0)
        cross = product(diag, upper) + product(slot_one, low_two, 0, 0)
        last = product(upper, cross, 0, 0) - product(low_two, slot_two, 0, 0)
        pieces, tall = parts.shape[0], parts.shape[1] // 3
        for n, term in enumerate((diag, cross, last)):
            parts[:, n * tall : (n + 1) * tall, :] = term.reshape(pieces, tall, width)


def level_blocks(info, gathered, other, low, pivot, rows):
    width = pivot.shape[-1]
    slots = other.shape[0]
    cols, piece = low.shape[0], width // low.shape[0]
    pieces = slots
    f32 = jnp.float32
    grid_spec = pltpu.PrefetchScalarGridSpec(
        num_scalar_prefetch=1,
        grid=(slots,),
        in_specs=[
            pl.BlockSpec((1, width, width), lambda r, s: (r, 0, s[r])),
            pl.BlockSpec((1, width, width), lambda r, s: (r, 0, 0)),
            pl.BlockSpec((cols, 2 * piece, width), lambda r, s: (0, r, 0)),
            pl.BlockSpec((cols, 2 * piece, width), lambda r, s: (0, s[10], 0)),
            pl.BlockSpec((cols, piece, width), lambda r, s: (0, 2 * slots, 0)),
            pl.BlockSpec((1, width, width), lambda r, s: (0, 0, 0)),
        ],
        out_specs=[
            pl.BlockSpec((2, width, width), lambda r, s: (0, 0, 0)),
            pl.BlockSpec((2, width, width), lambda r, s: (0, 0, 0)),
            pl.BlockSpec((pieces, 3 * width // pieces, width), lambda r, s: (0, 0, 0)),
        ],
        scratch_shapes=[pltpu.VMEM((2 * width, 2 * width), f32)],
    )
    return pl.pallas_call(
        kernel,
        grid_spec=grid_spec,
        out_shape=[
            jax.ShapeDtypeStruct((2, width, width), f32),
            jax.ShapeDtypeStruct((2, width, width), f32),
            jax.ShapeDtypeStruct((pieces, 3 * width // pieces, width), f32),
        ],
        compiler_params=pltpu.CompilerParams(vmem_limit_bytes=40 << 20),
        cost_estimate=pl.CostEstimate(flops=10_000_000_000, bytes_accessed=12_000_000, transcendentals=0),
    )(info, gathered, other, low, low, low, pivot)


def exchange(x, axis):
    return lax.all_to_all(x, axis, split_axis=0, concat_axis=0, tiled=True)


def swap(x):
    return lax.ppermute(x, CORES, [(0, 1), (1, 0)])


def body(anc, pattern, parents, low_one, pivot_one, low_two, factor, pivot_two):
    row, chip, core = (lax.axis_index(a) for a in (ROWS, CHIPS, CORES))
    rows, chips, cores = (lax.axis_size(a) for a in (ROWS, CHIPS, CORES))
    cols = chips * cores
    width = pivot_one.shape[-1]
    piece = width // cols
    col = chip * cores + core
    kind = jnp.arange(cols, dtype=jnp.int32)
    children = jnp.sum(jnp.where(parents[None, :] == kind[:, None], kind[None, :], 0), axis=1)

    gathered = lax.all_gather(anc, ROWS, axis=0, tiled=False)

    flat = [x.reshape(cols, piece, width) for x in (low_one, low_two, factor)]
    pieces = exchange(jnp.concatenate(flat, axis=1), (CHIPS, CORES)).reshape(3 * cols, piece, width)
    order = jnp.stack([3 * kind, 3 * children + 1], axis=1).reshape(-1)
    routed = jnp.take(pieces, order, axis=0).reshape(rows, cores * 2 * piece, width)
    uppers = jnp.take(pieces, 3 * lax.dynamic_slice_in_dim(children, row * cores, cores) + 2, axis=0)
    mine = exchange(routed, ROWS).reshape(rows, cores, 2 * piece, width)
    mine = mine.transpose(1, 0, 2, 3).reshape(cores, rows * 2 * piece, width)
    mine = jnp.concatenate([mine, uppers], axis=1)
    send = jnp.broadcast_to(mine[None], (chips, *mine.shape)).reshape(cols, *mine.shape[1:])
    low = exchange(send, (CHIPS, CORES))

    base = jnp.arange(rows, dtype=jnp.int32) * 2
    here = jnp.take(pattern, row * cores + core, axis=0)
    there = jnp.take(pattern, row * cores + 1 - core, axis=0)
    pick = (there - base)[:, None, None] > 0
    other = swap(jnp.where(pick, gathered[:, :, width:], gathered[:, :, :width]))
    on_slot = jnp.take(here, chip) != col
    info = jnp.concatenate(
        [here - base, jnp.stack([on_slot.astype(jnp.int32), (chip == row).astype(jnp.int32), chip])]
    )
    keep, give, parts = level_blocks(info, gathered, other, low, pivot_one, rows)
    taken = swap(give)

    summed = jnp.sum(exchange(parts, CHIPS), axis=0)
    halves = summed.reshape(3, cores, piece, width).transpose(1, 0, 2, 3).reshape(cores, 3 * piece, width)
    halves = jnp.broadcast_to(halves[None], (rows, *halves.shape)).reshape(cols, 3 * piece, width)
    known = exchange(halves, (ROWS, CORES)).reshape(3 * cols, piece, width)
    order = jnp.stack([3 * kind, 3 * parents + 1, 3 * parents + 2], axis=1).reshape(-1)
    final = exchange(jnp.take(known, order, axis=0).reshape(cols, 3 * piece, width), (CHIPS, CORES))
    final = final.reshape(cols, 3, piece, width)
    diag_one, cross, last = (final[:, n].reshape(1, width, width) for n in range(3))

    first = core == 0
    column_one = jnp.where(first, jnp.stack([keep[0], taken[0]]), jnp.stack([taken[0], keep[0]]))
    pair = jnp.stack([keep[1], taken[1]])
    every = lax.all_gather(pair, ROWS, axis=0, tiled=True)
    wanted = lax.dynamic_slice_in_dim(parents, row * cores, cores)
    column_two = jnp.take(every, 2 * (wanted // 2) + jnp.bitwise_xor(wanted % 2, core), axis=0)
    return column_one, diag_one, column_two, -cross, pivot_two + last


def solution(mesh):
    rows, cols = mesh.devices.shape
    cut = Mesh(mesh.devices.reshape(rows, cols // 2, 2), (ROWS, CHIPS, CORES))
    side = (CHIPS, CORES)
    return jax.shard_map(
        body,
        mesh=cut,
        in_specs=(
            P(side, ROWS),
            P(),
            P(),
            P(side, ROWS, None),
            P(side, None, None),
            P(side, ROWS, None),
            P(side, None, None),
            P(side, None, None),
        ),
        out_specs=(
            P(ROWS, side, None),
            P(side, None, None),
            P(ROWS, side, None),
            P(side, None, None),
            P(side, None, None),
        ),
        check_vma=False,
    )
```

```python
import functools

import jax
import jax.numpy as jnp
from jax import lax
from jax.experimental import pallas as pl
from jax.experimental.pallas import tpu as pltpu
from jax.sharding import Mesh, PartitionSpec as P

NEXT, RING, LINE, ACROSS, CORES = "next", "ring", "x", "across", "core"
ROWS = (NEXT, RING)
CHIPS = (LINE, ACROSS)
SIDE = (*CHIPS, CORES)


def split(x):
    high = x.astype(jnp.bfloat16)
    return high, (x - high.astype(jnp.float32)).astype(jnp.bfloat16)


def product(a, b, a_dim=1, b_dim=0):
    dims = (((a_dim,), (b_dim,)), ((), ()))
    dot = functools.partial(lax.dot_general, dimension_numbers=dims, preferred_element_type=jnp.float32)
    (ah, al), (bh, bl) = split(a), split(b)
    return dot(ah, bh) + (dot(ah, bl) + dot(al, bh))


ROUTE = (
    ((0, 0, 0), (0, 0, 1)),
    ((-1, 0, 0), (-1, 0, 1)),
    ((1, 0, 0), (1, 0, 1)),
    ((0, 1, 0), (0, 1, 1)),
    ((-1, 1, 0), (-1, 1, 1), (2, 0, 0)),
    ((1, 1, 0), (1, 1, 1), (2, 0, 1)),
    ((2, 1, 0),),
    ((2, 1, 1),),
)
PLACES = ((0, 0), (-1, 0), (1, 0), (2, 0), (0, 1), (-1, 1), (1, 1), (2, 1))


def kernel(info, own, other, *refs):
    lows, (pivot, keep, give, second, parts, total, wide) = refs[: len(ROUTE)], refs[len(ROUTE) :]
    step = pl.program_id(0)
    slots = pl.num_programs(0)
    width = own.shape[-1]
    piece = 16

    @pl.when(step == 0)
    def _():
        total[...] = jnp.zeros_like(total)

    def collect(row, levels):
        for ref, entries in zip(lows, ROUTE):
            for n, (along, beside, part) in enumerate(entries):
                chip = info[20 + PLACES.index((along, beside))]
                to = pl.ds(pl.multiple_of((2 * chip + part) * piece, piece), piece)
                for level in range(levels):
                    at = pl.ds(pl.multiple_of(row + level * piece, piece), piece)
                    wide[to, level * width : (level + 1) * width] = ref[n, at, :]

    left = jnp.concatenate([own[0], other[0]], axis=0)
    collect(2 * piece * info[12 + step], 2)
    total[...] += product(left, wide[...])

    @pl.when(step == slots - 1)
    def _():
        collect(2 * piece * slots, 1)
        upper = wide[:, :width]
        one = total[:, :width]
        two = product(one, upper) - total[:, width:]
        keep[0] = -one[:width]
        give[0] = -one[width:]
        core = info[11]
        tiles = (second.shape[0], second.shape[2], width)
        second[:, core] = two[:width].reshape(tiles)
        second[:, 1 - core] = two[width:].reshape(tiles)
        away = info[8] > 0
        slot_one = jnp.where(away, -one[width:], -one[:width])
        slot_two = jnp.where(away, two[width:], two[:width])
        collect(2 * piece * info[10], 2)
        low_one, low_two = wide[:, :width], wide[:, width:]
        here = jnp.where(info[9] > 0, pivot[0], jnp.zeros_like(slot_one))
        diag = here - product(low_one, slot_one, 0, 0)
        cross = product(diag, upper) + product(slot_one, low_two, 0, 0)
        last = product(upper, cross, 0, 0) - product(low_two, slot_two, 0, 0)
        pieces, tall = parts.shape[0], parts.shape[1] // 3
        for n, term in enumerate((diag, cross, last)):
            parts[:, n * tall : (n + 1) * tall, :] = term.reshape(pieces, tall, width)


def level_blocks(info, gathered, other, lows, pivot):
    width = pivot.shape[-1]
    slots = other.shape[0]
    pieces = slots
    f32 = jnp.float32
    grid_spec = pltpu.PrefetchScalarGridSpec(
        num_scalar_prefetch=1,
        grid=(slots,),
        in_specs=[
            pl.BlockSpec((1, width, width), lambda r, s: (r, 0, s[r])),
            pl.BlockSpec((1, width, width), lambda r, s: (r, 0, 0)),
            *[pl.BlockSpec(x.shape, lambda r, s: (0, 0, 0), pipeline_mode=pl.Buffered(1)) for x in lows],
            pl.BlockSpec((1, width, width), lambda r, s: (0, 0, 0)),
        ],
        out_specs=[
            pl.BlockSpec((1, width, width), lambda r, s: (0, 0, 0)),
            pl.BlockSpec((1, width, width), lambda r, s: (0, 0, 0)),
            pl.BlockSpec((slots, 2, width // slots, width), lambda r, s: (0, 0, 0, 0)),
            pl.BlockSpec((pieces, 3 * width // pieces, width), lambda r, s: (0, 0, 0)),
        ],
        scratch_shapes=[pltpu.VMEM((2 * width, 2 * width), f32), pltpu.VMEM((width, 2 * width), f32)],
    )
    return pl.pallas_call(
        kernel,
        grid_spec=grid_spec,
        out_shape=[
            jax.ShapeDtypeStruct((1, width, width), f32),
            jax.ShapeDtypeStruct((1, width, width), f32),
            jax.ShapeDtypeStruct((slots, 2, width // slots, width), f32),
            jax.ShapeDtypeStruct((pieces, 3 * width // pieces, width), f32),
        ],
        compiler_params=pltpu.CompilerParams(vmem_limit_bytes=60 << 20),
        cost_estimate=pl.CostEstimate(flops=10_000_000_000, bytes_accessed=12_000_000, transcendentals=0),
    )(info, gathered, other, *lows, pivot)


def exchange(x, axis):
    return lax.all_to_all(x, axis, split_axis=0, concat_axis=0, tiled=True)


def swap(x, axis=CORES):
    return lax.ppermute(x, axis, [(0, 1), (1, 0)])


def shift(x, axis, by):
    n = lax.axis_size(axis)
    return lax.ppermute(x, axis, [(i, (i + by) % n) for i in range(n)])


def go_round(*ways):
    hold = lax.optimization_barrier
    owns = hold(tuple(own for own, _, _ in ways))
    near = []
    for own, (_, line, neighbour) in zip(owns, ways):
        near.append((shift(own, line, 1), shift(own, line, -1), swap(own, neighbour)))
    near = hold(near)
    far = []
    for (below, above, beside), (_, line, _) in zip(near, ways):
        half = below.shape[0] // 2
        up = shift(jnp.concatenate([beside, below[:half]]), line, 1)
        down = shift(jnp.concatenate([beside, above[half:]]), line, -1)
        far.append((up, down))
    far = hold(far)
    ends = []
    for (up, down), (own, line, _) in zip(far, ways):
        half = own.shape[0] // 2
        ends.append((shift(up[:half], line, 1), shift(down[half : 2 * half], line, -1)))
    return [(own, *n, *f, *e) for own, n, f, e in zip(owns, near, far, ends)]


def body(anc, pattern, parents, low_one, pivot_one, low_two, factor, pivot_two):
    row, line, across, core = (lax.axis_index(a) for a in (ROWS, LINE, ACROSS, CORES))
    half = lax.axis_index(NEXT)
    rows, lines, pair, cores = (lax.axis_size(a) for a in (ROWS, LINE, ACROSS, CORES))
    chips = lines * pair
    cols = chips * cores
    width = pivot_one.shape[-1]
    piece = width // cols
    chip = line * pair + across
    col = chip * cores + core
    kind = jnp.arange(cols, dtype=jnp.int32)
    children = jnp.sum(jnp.where(parents[None, :] == kind[:, None], kind[None, :], 0), axis=1)

    flat = [x.reshape(cols, piece, width) for x in (low_one, low_two, factor)]
    pieces = exchange(jnp.concatenate(flat, axis=1), SIDE).reshape(3 * cols, piece, width)
    order = jnp.stack([3 * kind, 3 * children + 1], axis=1).reshape(-1)
    routed = jnp.take(pieces, order, axis=0).reshape(rows, cores * 2 * piece, width)
    own_children = lax.dynamic_slice_in_dim(children, row * cores, cores)
    uppers = jnp.take(pieces, 3 * own_children + 2, axis=0)
    mine = exchange(routed, ROWS).reshape(rows, cores, 2 * piece, width)

    kept, sent = (
        jnp.concatenate(
            [
                lax.dynamic_index_in_dim(mine, n, 1, keepdims=False).reshape(rows * 2 * piece, width),
                lax.dynamic_index_in_dim(uppers, n, 0, keepdims=False),
            ]
        )
        for n in (core, 1 - core)
    )
    got = swap(sent)
    both = jnp.where(core == 0, jnp.stack([kept, got]), jnp.stack([got, kept]))

    inverse, lows = go_round((anc, RING, NEXT), (both, LINE, ACROSS))
    own, below, above, beside, up, down, low_far, high_far = inverse
    across_far = jnp.concatenate([up[width:], down[width:]])
    last_far = jnp.concatenate([low_far, high_far])
    gathered = jnp.stack([own, below, above, across_far, beside, up[:width], down[:width], last_far])

    ring = lax.axis_index(RING)
    lengths = lax.axis_size(RING)
    slot = jnp.stack([(half ^ n) * lengths + (ring + m) % lengths for m, n in PLACES])
    places = jnp.stack([(line + m) % lines * pair + (across ^ n) for m, n in PLACES])
    here = jnp.take(pattern, row * cores + core, axis=0)
    there = jnp.take(pattern, row * cores + 1 - core, axis=0)
    pick = jnp.take(there, slot)[:, None, None] % 2 > 0
    other = swap(jnp.where(pick, gathered[:, :, width:], gathered[:, :, :width]))
    away = jnp.take(here, chip) != col
    flags = jnp.stack([away.astype(jnp.int32), (chip == row).astype(jnp.int32), chip, core])
    info = jnp.concatenate([jnp.take(here, slot) % 2, flags, slot, places])
    keep, give, second, parts = level_blocks(info, gathered, other, lows, pivot_one)
    taken = swap(give)
    column_one = jnp.where(core == 0, jnp.concatenate([keep, taken]), jnp.concatenate([taken, keep]))

    summed = jnp.sum(exchange(parts, CHIPS), axis=0)
    halves = summed.reshape(3, cores, piece, width).transpose(1, 0, 2, 3).reshape(1, cores, 3 * piece, width)
    halves = jnp.broadcast_to(halves, (rows, *halves.shape[1:]))
    send = jnp.concatenate([halves, second], axis=2).reshape(cols, -1, width)
    known = exchange(send, (*ROWS, CORES))
    column_two = jnp.take(known[:, 3 * piece :], parents, axis=0)
    column_two = exchange(column_two.reshape(rows, -1, width), ROWS)
    column_two = column_two.reshape(rows, cores, -1, width).transpose(1, 0, 2, 3)
    known = known.reshape(cols, -1, piece, width)
    blocks = [known[:, 0], jnp.take(known[:, 1:3], parents, axis=0).reshape(cols, -1, width)]
    final = exchange(jnp.concatenate(blocks, axis=1), SIDE)
    final = final.reshape(cols, 3, piece, width)
    diag_one, cross, last = (final[:, n].reshape(1, width, width) for n in range(3))
    return column_one, diag_one, column_two.reshape(cores, width, width), -cross, pivot_two + last


def solution(mesh):
    rows, cols = mesh.devices.shape
    cut = Mesh(mesh.devices.reshape(2, rows // 2, cols // 4, 2, 2), (*ROWS, *SIDE))
    flat, wide = P(SIDE, None, None), P(SIDE, ROWS, None)
    return jax.shard_map(
        body,
        mesh=cut,
        in_specs=(P(SIDE, ROWS), P(), P(), wide, flat, wide, flat, flat),
        out_specs=(P(ROWS, SIDE, None), flat, P(ROWS, SIDE, None), flat, flat),
        check_vma=False,
    )
```

```python
import functools

import jax
import jax.numpy as jnp
from jax import lax
from jax.experimental import pallas as pl
from jax.experimental.pallas import tpu as pltpu
from jax.sharding import Mesh, PartitionSpec as P

NEXT, RING, LINE, ACROSS, CORES = "next", "ring", "x", "across", "core"
ROWS = (NEXT, RING)
CHIPS = (LINE, ACROSS)
SIDE = (*CHIPS, CORES)


def split(x):
    high = x.astype(jnp.bfloat16)
    return high, (x - high.astype(jnp.float32)).astype(jnp.bfloat16)


def product(a, b, a_dim=1, b_dim=0):
    (ah, al), (bh, bl) = split(a), split(b)
    left = jnp.concatenate([ah, ah, al], axis=a_dim)
    right = jnp.concatenate([bh, bl, bh], axis=b_dim)
    dims = (((a_dim,), (b_dim,)), ((), ()))
    return lax.dot_general(left, right, dims, preferred_element_type=jnp.float32)


ROUTE = (
    ((0, 0, 0), (0, 0, 1)),
    ((-1, 0, 0), (-1, 0, 1)),
    ((1, 0, 0), (1, 0, 1)),
    ((0, 1, 0), (0, 1, 1)),
    ((-1, 1, 0), (-1, 1, 1), (2, 0, 0)),
    ((1, 1, 0), (1, 1, 1), (2, 0, 1)),
    ((2, 1, 0),),
    ((2, 1, 1),),
)
PLACES = ((0, 0), (-1, 0), (1, 0), (0, 1), (-1, 1), (1, 1), (2, 0), (2, 1))


def kernel(info, *refs):
    arrivals, refs = refs[: len(ROUTE)], refs[len(ROUTE) :]
    given, refs = refs[:3], refs[3:]
    lows, refs = refs[: len(ROUTE)], refs[len(ROUTE) :]
    pivot, keep, give, second, parts, total, left, right, low_done, left_done = refs
    slots, width = left.shape[0], left.shape[-1]

    low_copies = []
    for ref, entries in zip(lows, ROUTE):
        for n, (along, beside, part) in enumerate(entries):
            col = 2 * info[20 + PLACES.index((along, beside))] + part
            done = low_done.at[len(low_copies)]
            low_copies.append(pltpu.make_async_copy(ref.at[n], right.at[:, col], done))
    left_copies = [[] for _ in range(slots)]
    parts_of = width // 2
    for which, (ref, entries) in enumerate(zip(arrivals, ROUTE)):
        for n, (along, beside, part) in enumerate(entries):
            t = PLACES.index((along, beside))
            half = pl.ds(pl.multiple_of(info[t] * width, width), width)
            source = ref.at[pl.ds(n * parts_of, parts_of), half]
            target = left.at[t, pl.ds(part * parts_of, parts_of)]
            left_copies[t].append(pltpu.make_async_copy(source, target, left_done.at[t, part]))
    for t in range(slots):
        group = 0 if t < 4 else 1 if t < 7 else 2
        source = given[group].at[t - (0, 4, 7)[group]]
        left_copies[t].append(pltpu.make_async_copy(source, left.at[t, pl.ds(width, width)], left_done.at[t, 2]))
    for copy in low_copies:
        copy.start()
    for copies in left_copies:
        for copy in copies:
            copy.start()
    for copy in low_copies:
        copy.wait()

    def low(row):
        return [right[2 * row + n].reshape(width, width) for n in range(2)]

    for t in range(slots):
        for copy in left_copies[t]:
            copy.wait()
        term = product(left[t], jnp.concatenate(low(info[12 + t]), axis=1))
        if t == 0:
            total[...] = term
        else:
            total[...] += term

    upper = right[2 * slots].reshape(width, width)
    one = total[:, :width]
    two = product(one, upper) - total[:, width:]
    keep[0] = -one[:width]
    give[0] = -one[width:]
    core = info[11]
    tiles = (second.shape[0], second.shape[2], width)
    second[:, core] = two[:width].reshape(tiles)
    second[:, 1 - core] = two[width:].reshape(tiles)
    away = info[8] > 0
    slot_one = jnp.where(away, -one[width:], -one[:width])
    slot_two = jnp.where(away, two[width:], two[:width])
    low_one, low_two = low(info[10])
    here = jnp.where(info[9] > 0, pivot[0], jnp.zeros_like(slot_one))
    diag = here - product(low_one, slot_one, 0, 0)
    cross = product(diag, upper) + product(slot_one, low_two, 0, 0)
    last = product(upper, cross, 0, 0) - product(low_two, slot_two, 0, 0)
    pieces, tall = parts.shape[0], parts.shape[1] // 3
    for n, term in enumerate((diag, cross, last)):
        parts[:, n * tall : (n + 1) * tall, :] = term.reshape(pieces, tall, width)


def level_blocks(info, arrivals, given, lows, pivot):
    width = pivot.shape[-1]
    slots = len(PLACES)
    pieces = slots
    cols = 2 * slots
    f32 = jnp.float32
    whole = lambda *shape: pl.BlockSpec(shape, lambda i, s: (0,) * len(shape))
    grid_spec = pltpu.PrefetchScalarGridSpec(
        num_scalar_prefetch=1,
        grid=(1,),
        in_specs=[pl.BlockSpec(memory_space=pl.ANY)] * (2 * len(ROUTE) + 3) + [whole(1, width, width)],
        out_specs=[
            whole(1, width, width),
            whole(1, width, width),
            whole(slots, 2, width // slots, width),
            whole(pieces, 3 * width // pieces, width),
        ],
        scratch_shapes=[
            pltpu.VMEM((2 * width, 2 * width), f32),
            pltpu.VMEM((slots, 2 * width, width), f32),
            pltpu.VMEM((2 * slots + 1, cols, width // cols, width), f32),
            pltpu.SemaphoreType.DMA((cols,)),
            pltpu.SemaphoreType.DMA((slots, 3)),
        ],
    )
    return pl.pallas_call(
        kernel,
        grid_spec=grid_spec,
        out_shape=[
            jax.ShapeDtypeStruct((1, width, width), f32),
            jax.ShapeDtypeStruct((1, width, width), f32),
            jax.ShapeDtypeStruct((slots, 2, width // slots, width), f32),
            jax.ShapeDtypeStruct((pieces, 3 * width // pieces, width), f32),
        ],
        compiler_params=pltpu.CompilerParams(vmem_limit_bytes=60 << 20),
        cost_estimate=pl.CostEstimate(flops=10_000_000_000, bytes_accessed=12_000_000, transcendentals=0),
    )(info, *arrivals, *given, *lows, pivot)


def exchange(x, axis):
    return lax.all_to_all(x, axis, split_axis=0, concat_axis=0, tiled=True)


def swap(x, axis=CORES):
    return lax.ppermute(x, axis, [(0, 1), (1, 0)])


def shift(x, axis, by):
    n = lax.axis_size(axis)
    return lax.ppermute(x, axis, [(i, (i + by) % n) for i in range(n)])


def go_round(*ways):
    hold = lax.optimization_barrier
    owns = hold(tuple(own for own, _, _ in ways))
    near = []
    for own, (_, line, neighbour) in zip(owns, ways):
        near.append((shift(own, line, 1), shift(own, line, -1), swap(own, neighbour)))
    near = hold(near)
    far = []
    for (below, above, beside), (_, line, _) in zip(near, ways):
        half = below.shape[0] // 2
        up = shift(jnp.concatenate([beside, below[:half]]), line, 1)
        down = shift(jnp.concatenate([beside, above[half:]]), line, -1)
        far.append((up, down))
    far = hold(far)
    ends = []
    for (up, down), (own, line, _) in zip(far, ways):
        half = own.shape[0] // 2
        ends.append((shift(up[:half], line, 1), shift(down[half : 2 * half], line, -1)))
    return [(own, *n, *f, *e) for own, n, f, e in zip(owns, near, far, ends)]


def body(anc, pattern, parents, low_one, pivot_one, low_two, factor, pivot_two):
    row, line, across, core = (lax.axis_index(a) for a in (ROWS, LINE, ACROSS, CORES))
    half = lax.axis_index(NEXT)
    rows, lines, pair, cores = (lax.axis_size(a) for a in (ROWS, LINE, ACROSS, CORES))
    chips = lines * pair
    cols = chips * cores
    width = pivot_one.shape[-1]
    piece = width // cols
    chip = line * pair + across
    col = chip * cores + core
    kind = jnp.arange(cols, dtype=jnp.int32)
    children = jnp.sum(jnp.where(parents[None, :] == kind[:, None], kind[None, :], 0), axis=1)

    flat = [x.reshape(cols, piece, width) for x in (low_one, low_two, factor)]
    pieces = exchange(jnp.concatenate(flat, axis=1), SIDE).reshape(3 * cols, piece, width)
    order = jnp.stack([3 * kind, 3 * children + 1], axis=1).reshape(-1)
    routed = jnp.take(pieces, order, axis=0).reshape(rows, cores * 2 * piece, width)
    own_children = lax.dynamic_slice_in_dim(children, row * cores, cores)
    uppers = jnp.take(pieces, 3 * own_children + 2, axis=0)
    upper = swap(lax.dynamic_index_in_dim(uppers, 1 - core, 0))
    kept = lax.dynamic_index_in_dim(uppers, core, 0)
    uppers = jnp.where(core == 0, jnp.stack([kept, upper]), jnp.stack([upper, kept]))
    mine = exchange(routed.reshape(cols, 2 * piece, width), (*ROWS, CORES))
    mine = mine.reshape(rows, cores, 2, piece, width).transpose(1, 0, 2, 3, 4)
    both = jnp.concatenate([mine.reshape(cores, rows * 2, piece, width), uppers], axis=1)

    inverse, lows = go_round((anc, RING, NEXT), (both, LINE, ACROSS))
    ring = lax.axis_index(RING)
    lengths = lax.axis_size(RING)
    slot = jnp.stack([(half ^ n) * lengths + (ring + m) % lengths for m, n in PLACES])
    places = jnp.stack([(line + m) % lines * pair + (across ^ n) for m, n in PLACES])
    here = jnp.take(pattern, row * cores + core, axis=0)
    there = jnp.take(pattern, row * cores + 1 - core, axis=0)
    picks = jnp.take(there, slot) % 2 > 0

    def handed(first, *blocks):
        picked = [jnp.where(picks[first + n], x[:, width:], x[:, :width]) for n, x in enumerate(blocks)]
        return swap(jnp.stack(picked))

    own, below, above, beside, up, down, low_far, high_far = inverse
    given = (
        handed(0, own, below, above, beside),
        handed(4, up[:width], down[:width], jnp.concatenate([up[width:], down[width:]])),
        handed(7, jnp.concatenate([low_far, high_far])),
    )
    away = jnp.take(here, chip) != col
    flags = jnp.stack([away.astype(jnp.int32), (chip == row).astype(jnp.int32), chip, core])
    info = jnp.concatenate([jnp.take(here, slot) % 2, flags, slot, places])
    keep, give, second, parts = level_blocks(info, inverse, given, lows, pivot_one)
    taken = swap(give)
    column_one = jnp.where(core == 0, jnp.concatenate([keep, taken]), jnp.concatenate([taken, keep]))

    summed = jnp.sum(exchange(parts, CHIPS), axis=0)
    halves = summed.reshape(3, cores, piece, width).transpose(1, 0, 2, 3).reshape(1, cores, 3 * piece, width)
    halves = jnp.broadcast_to(halves, (rows, *halves.shape[1:]))
    send = jnp.concatenate([halves, second], axis=2).reshape(cols, -1, width)
    known = exchange(send, (*ROWS, CORES))
    column_two = jnp.take(known[:, 3 * piece :], parents, axis=0)
    column_two = exchange(column_two.reshape(rows, -1, width), ROWS)
    column_two = column_two.reshape(rows, cores, -1, width).transpose(1, 0, 2, 3)
    known = known.reshape(cols, -1, piece, width)
    blocks = [known[:, 0], jnp.take(known[:, 1:3], parents, axis=0).reshape(cols, -1, width)]
    final = exchange(jnp.concatenate(blocks, axis=1), SIDE)
    final = final.reshape(cols, 3, piece, width)
    diag_one, cross, last = (final[:, n].reshape(1, width, width) for n in range(3))
    return column_one, diag_one, column_two.reshape(cores, width, width), -cross, pivot_two + last


def solution(mesh):
    rows, cols = mesh.devices.shape
    cut = Mesh(mesh.devices.reshape(2, rows // 2, cols // 4, 2, 2), (*ROWS, *SIDE))
    flat, wide = P(SIDE, None, None), P(SIDE, ROWS, None)
    return jax.shard_map(
        body,
        mesh=cut,
        in_specs=(P(SIDE, ROWS), P(), P(), wide, flat, wide, flat, flat),
        out_specs=(P(ROWS, SIDE, None), flat, P(ROWS, SIDE, None), flat, flat),
        check_vma=False,
    )
```

```python
import functools

import jax
import jax.numpy as jnp
from jax import lax
from jax.experimental import pallas as pl
from jax.experimental.pallas import tpu as pltpu
from jax.sharding import Mesh, PartitionSpec as P

NEXT, RING, LINE, ACROSS, CORES = "next", "ring", "x", "across", "core"
ROWS = (NEXT, RING)
CHIPS = (LINE, ACROSS)
SIDE = (*CHIPS, CORES)


def split(x):
    high = x.astype(jnp.bfloat16)
    return high, (x - high.astype(jnp.float32)).astype(jnp.bfloat16)


def product(a, b, a_dim=1, b_dim=0):
    (ah, al), (bh, bl) = split(a), split(b)
    left = jnp.concatenate([ah, ah, al], axis=a_dim)
    right = jnp.concatenate([bh, bl, bh], axis=b_dim)
    dims = (((a_dim,), (b_dim,)), ((), ()))
    return lax.dot_general(left, right, dims, preferred_element_type=jnp.float32)


ROUTE = (
    ((0, 0, 0), (0, 0, 1)),
    ((-1, 0, 0), (-1, 0, 1)),
    ((1, 0, 0), (1, 0, 1)),
    ((0, 1, 0), (0, 1, 1)),
    ((-1, 1, 0), (-1, 1, 1), (2, 0, 0)),
    ((1, 1, 0), (1, 1, 1), (2, 0, 1)),
    ((2, 1, 0),),
    ((2, 1, 1),),
)
PLACES = ((0, 0), (-1, 0), (1, 0), (0, 1), (-1, 1), (1, 1), (2, 0), (2, 1))


def kernel(info, *refs):
    arrivals, refs = refs[: len(ROUTE)], refs[len(ROUTE) :]
    given, refs = refs[:3], refs[3:]
    lows, refs = refs[: len(ROUTE)], refs[len(ROUTE) :]
    pivot, keep, give, second, parts, total, left, right, low_done, left_done = refs
    slots, width = left.shape[0], left.shape[-1]

    low_copies = []
    for ref, entries in zip(lows, ROUTE):
        for n, (along, beside, part) in enumerate(entries):
            col = 2 * info[20 + PLACES.index((along, beside))] + part
            done = low_done.at[len(low_copies)]
            low_copies.append(pltpu.make_async_copy(ref.at[n], right.at[:, col], done))
    left_copies = [[] for _ in range(slots)]
    parts_of = width // 2
    for which, (ref, entries) in enumerate(zip(arrivals, ROUTE)):
        for n, (along, beside, part) in enumerate(entries):
            t = PLACES.index((along, beside))
            half = pl.ds(pl.multiple_of(info[t] * width, width), width)
            source = ref.at[pl.ds(n * parts_of, parts_of), half]
            target = left.at[t, pl.ds(part * parts_of, parts_of)]
            left_copies[t].append(pltpu.make_async_copy(source, target, left_done.at[t, part]))
    for t in range(slots):
        group = 0 if t < 4 else 1 if t < 7 else 2
        source = given[group].at[t - (0, 4, 7)[group]]
        left_copies[t].append(pltpu.make_async_copy(source, left.at[t, pl.ds(width, width)], left_done.at[t, 2]))
    for copy in low_copies:
        copy.start()
    for copies in left_copies:
        for copy in copies:
            copy.start()
    for copy in low_copies:
        copy.wait()

    def low(row):
        return [right[2 * row + n].reshape(width, width) for n in range(2)]

    for t in range(0, slots, 2):
        for copy in left_copies[t] + left_copies[t + 1]:
            copy.wait()
        block = jnp.concatenate([jnp.concatenate(low(info[12 + t + n]), axis=1) for n in range(2)], axis=0)
        term = product(jnp.concatenate([left[t], left[t + 1]], axis=1), block)
        if t == 0:
            total[...] = term
        else:
            total[...] += term

    upper = right[2 * slots].reshape(width, width)
    one = total[:, :width]
    two = product(one, upper) - total[:, width:]
    keep[0] = -one[:width]
    give[0] = -one[width:]
    core = info[11]
    tiles = (second.shape[0], second.shape[2], width)
    second[:, core] = two[:width].reshape(tiles)
    second[:, 1 - core] = two[width:].reshape(tiles)
    away = info[8] > 0
    slot_one = jnp.where(away, -one[width:], -one[:width])
    slot_two = jnp.where(away, two[width:], two[:width])
    low_one, low_two = low(info[10])
    here = jnp.where(info[9] > 0, pivot[0], jnp.zeros_like(slot_one))
    diag = here - product(low_one, slot_one, 0, 0)
    cross = product(diag, upper) + product(slot_one, low_two, 0, 0)
    last = product(upper, cross, 0, 0) - product(low_two, slot_two, 0, 0)
    pieces, tall = parts.shape[0], parts.shape[1] // 3
    for n, term in enumerate((diag, cross, last)):
        parts[:, n * tall : (n + 1) * tall, :] = term.reshape(pieces, tall, width)


def level_blocks(info, arrivals, given, lows, pivot):
    width = pivot.shape[-1]
    slots = len(PLACES)
    pieces = slots
    cols = 2 * slots
    f32 = jnp.float32
    whole = lambda *shape: pl.BlockSpec(shape, lambda i, s: (0,) * len(shape))
    grid_spec = pltpu.PrefetchScalarGridSpec(
        num_scalar_prefetch=1,
        grid=(1,),
        in_specs=[pl.BlockSpec(memory_space=pl.ANY)] * (2 * len(ROUTE) + 3) + [whole(1, width, width)],
        out_specs=[
            whole(1, width, width),
            whole(1, width, width),
            whole(slots, 2, width // slots, width),
            whole(pieces, 3 * width // pieces, width),
        ],
        scratch_shapes=[
            pltpu.VMEM((2 * width, 2 * width), f32),
            pltpu.VMEM((slots, 2 * width, width), f32),
            pltpu.VMEM((2 * slots + 1, cols, width // cols, width), f32),
            pltpu.SemaphoreType.DMA((cols,)),
            pltpu.SemaphoreType.DMA((slots, 3)),
        ],
    )
    return pl.pallas_call(
        kernel,
        grid_spec=grid_spec,
        out_shape=[
            jax.ShapeDtypeStruct((1, width, width), f32),
            jax.ShapeDtypeStruct((1, width, width), f32),
            jax.ShapeDtypeStruct((slots, 2, width // slots, width), f32),
            jax.ShapeDtypeStruct((pieces, 3 * width // pieces, width), f32),
        ],
        compiler_params=pltpu.CompilerParams(vmem_limit_bytes=28 << 20),
        cost_estimate=pl.CostEstimate(flops=10_000_000_000, bytes_accessed=12_000_000, transcendentals=0),
    )(info, *arrivals, *given, *lows, pivot)


def exchange(x, axis):
    return lax.all_to_all(x, axis, split_axis=0, concat_axis=0, tiled=True)


def pick(x, index):
    return x.at[index].get(mode="promise_in_bounds")


def swap(x, axis=CORES):
    return lax.ppermute(x, axis, [(0, 1), (1, 0)])


def shift(x, axis, by):
    n = lax.axis_size(axis)
    return lax.ppermute(x, axis, [(i, (i + by) % n) for i in range(n)])


def go_round(*ways):
    hold = lax.optimization_barrier
    owns = hold(tuple(own for own, _, _ in ways))
    near = []
    for own, (_, line, neighbour) in zip(owns, ways):
        near.append((shift(own, line, 1), shift(own, line, -1), swap(own, neighbour)))
    near = hold(near)
    far = []
    for (below, above, beside), (_, line, _) in zip(near, ways):
        half = below.shape[0] // 2
        up = shift(jnp.concatenate([beside, below[:half]]), line, 1)
        down = shift(jnp.concatenate([beside, above[half:]]), line, -1)
        far.append((up, down))
    far = hold(far)
    ends = []
    for (up, down), (own, line, _) in zip(far, ways):
        half = own.shape[0] // 2
        ends.append((shift(up[:half], line, 1), shift(down[half : 2 * half], line, -1)))
    return [(own, *n, *f, *e) for own, n, f, e in zip(owns, near, far, ends)]


def body(anc, pattern, parents, low_one, pivot_one, low_two, factor, pivot_two):
    row, line, across, core = (lax.axis_index(a) for a in (ROWS, LINE, ACROSS, CORES))
    half = lax.axis_index(NEXT)
    rows, lines, pair, cores = (lax.axis_size(a) for a in (ROWS, LINE, ACROSS, CORES))
    chips = lines * pair
    cols = chips * cores
    width = pivot_one.shape[-1]
    piece = width // cols
    chip = line * pair + across
    col = chip * cores + core
    kind = jnp.arange(cols, dtype=jnp.int32)
    children = jnp.sum(jnp.where(parents[None, :] == kind[:, None], kind[None, :], 0), axis=1)

    flat = [x.reshape(cols, piece, width) for x in (low_one, low_two, factor)]
    pieces = exchange(jnp.concatenate(flat, axis=1), SIDE).reshape(3 * cols, piece, width)
    order = jnp.stack([3 * kind, 3 * children + 1], axis=1).reshape(-1)
    routed = pick(pieces, order).reshape(rows, cores * 2 * piece, width)
    own_children = lax.dynamic_slice_in_dim(children, row * cores, cores)
    uppers = pick(pieces, 3 * own_children + 2)
    upper = swap(lax.dynamic_index_in_dim(uppers, 1 - core, 0))
    kept = lax.dynamic_index_in_dim(uppers, core, 0)
    uppers = jnp.where(core == 0, jnp.stack([kept, upper]), jnp.stack([upper, kept]))
    mine = exchange(routed.reshape(cols, 2 * piece, width), (*ROWS, CORES))
    mine = mine.reshape(rows, cores, 2, piece, width).transpose(1, 0, 2, 3, 4)
    both = jnp.concatenate([mine.reshape(cores, rows * 2, piece, width), uppers], axis=1)

    ring = lax.axis_index(RING)
    lengths = lax.axis_size(RING)
    slot = jnp.stack([(half ^ n) * lengths + (ring + m) % lengths for m, n in PLACES])
    places = jnp.stack([(line + m) % lines * pair + (across ^ n) for m, n in PLACES])
    here = pick(pattern, row * cores + core)
    picks = pick(pick(pattern, row * cores + 1 - core), slot) % 2 > 0
    away = pick(here, chip) != col
    flags = jnp.stack([away.astype(jnp.int32), (chip == row).astype(jnp.int32), chip, core])
    info = jnp.concatenate([pick(here, slot) % 2, flags, slot, places])
    info, picks, anc, both = lax.optimization_barrier((info, picks, anc, both))

    inverse, lows = go_round((anc, RING, NEXT), (both, LINE, ACROSS))

    def handed(first, *blocks):
        picked = [jnp.where(picks[first + n], x[:, width:], x[:, :width]) for n, x in enumerate(blocks)]
        return swap(jnp.stack(picked))

    own, below, above, beside, up, down, low_far, high_far = inverse
    given = (
        handed(0, own, below, above, beside),
        handed(4, up[:width], down[:width], jnp.concatenate([up[width:], down[width:]])),
        handed(7, jnp.concatenate([low_far, high_far])),
    )
    keep, give, second, parts = level_blocks(info, inverse, given, lows, pivot_one)
    taken = swap(give)
    column_one = jnp.where(core == 0, jnp.concatenate([keep, taken]), jnp.concatenate([taken, keep]))

    summed = jnp.sum(exchange(parts, CHIPS), axis=0)
    halves = summed.reshape(3, cores, piece, width).transpose(1, 0, 2, 3).reshape(1, cores, 3 * piece, width)
    halves = jnp.broadcast_to(halves, (rows, *halves.shape[1:]))
    send = jnp.concatenate([halves, second], axis=2).reshape(cols, -1, width)
    known = exchange(send, (*ROWS, CORES))
    column_two = pick(known[:, 3 * piece :], parents)
    column_two = exchange(column_two.reshape(rows, -1, width), ROWS)
    column_two = column_two.reshape(rows, cores, -1, width).transpose(1, 0, 2, 3)
    known = known.reshape(cols, -1, piece, width)
    blocks = [known[:, 0], pick(known[:, 1:3], parents).reshape(cols, -1, width)]
    final = exchange(jnp.concatenate(blocks, axis=1), SIDE)
    final = final.reshape(cols, 3, piece, width)
    diag_one, cross, last = (final[:, n].reshape(1, width, width) for n in range(3))
    return column_one, diag_one, column_two.reshape(cores, width, width), -cross, pivot_two + last


def solution(mesh):
    rows, cols = mesh.devices.shape
    cut = Mesh(mesh.devices.reshape(2, rows // 2, cols // 4, 2, 2), (*ROWS, *SIDE))
    flat, wide = P(SIDE, None, None), P(SIDE, ROWS, None)
    return jax.shard_map(
        body,
        mesh=cut,
        in_specs=(P(SIDE, ROWS), P(), P(), wide, flat, wide, flat, flat),
        out_specs=(P(ROWS, SIDE, None), flat, P(ROWS, SIDE, None), flat, flat),
        check_vma=False,
    )
```

```python
import functools

import jax
import jax.numpy as jnp
from jax import lax
from jax.experimental import pallas as pl
from jax.experimental.pallas import tpu as pltpu
from jax.sharding import Mesh, PartitionSpec as P

NEXT, RING, LINE, ACROSS, CORES = "next", "ring", "x", "across", "core"
ROWS = (NEXT, RING)
CHIPS = (LINE, ACROSS)
SIDE = (*CHIPS, CORES)


def split(x):
    high = x.astype(jnp.bfloat16)
    return high, (x - high.astype(jnp.float32)).astype(jnp.bfloat16)


def product(a, b, a_dim=1, b_dim=0):
    (ah, al), (bh, bl) = split(a), split(b)
    left = jnp.concatenate([ah, ah, al], axis=a_dim)
    right = jnp.concatenate([bh, bl, bh], axis=b_dim)
    dims = (((a_dim,), (b_dim,)), ((), ()))
    return lax.dot_general(left, right, dims, preferred_element_type=jnp.float32)


ROUTE = (
    ((0, 0, 0), (0, 0, 1)),
    ((-1, 0, 0), (-1, 0, 1)),
    ((1, 0, 0), (1, 0, 1)),
    ((2, 0, 0),),
    ((2, 0, 1),),
    ((0, 1, 0), (0, 1, 1)),
    ((-1, 1, 0), (-1, 1, 1)),
    ((1, 1, 0), (1, 1, 1)),
    ((2, 1, 0),),
    ((2, 1, 1),),
)
PLACES = ((0, 0), (-1, 0), (1, 0), (2, 0), (0, 1), (-1, 1), (1, 1), (2, 1))
GROUPS = (0, 5, 7)


def kernel(info, *refs):
    arrivals, refs = refs[: len(ROUTE)], refs[len(ROUTE) :]
    given, refs = refs[:3], refs[3:]
    lows, refs = refs[: len(ROUTE)], refs[len(ROUTE) :]
    pivot, keep, give, second, parts, total, left, right, low_done, left_done = refs
    slots, width = left.shape[0], left.shape[-1]

    low_copies = []
    for ref, entries in zip(lows, ROUTE):
        for n, (along, beside, part) in enumerate(entries):
            col = 2 * info[20 + PLACES.index((along, beside))] + part
            done = low_done.at[len(low_copies)]
            low_copies.append(pltpu.make_async_copy(ref.at[n], right.at[:, col], done))
    left_copies = [[] for _ in range(slots)]
    parts_of = width // 2
    for which, (ref, entries) in enumerate(zip(arrivals, ROUTE)):
        for n, (along, beside, part) in enumerate(entries):
            t = PLACES.index((along, beside))
            half = pl.ds(pl.multiple_of(info[t] * width, width), width)
            source = ref.at[pl.ds(n * parts_of, parts_of), half]
            target = left.at[t, pl.ds(part * parts_of, parts_of)]
            left_copies[t].append(pltpu.make_async_copy(source, target, left_done.at[t, part]))
    for t in range(slots):
        group = sum(t >= first for first in GROUPS) - 1
        source = given[group].at[t - GROUPS[group]]
        left_copies[t].append(pltpu.make_async_copy(source, left.at[t, pl.ds(width, width)], left_done.at[t, 2]))
    for copy in low_copies:
        copy.start()
    for copies in left_copies:
        for copy in copies:
            copy.start()
    for copy in low_copies:
        copy.wait()

    def low(row):
        return [right[2 * row + n].reshape(width, width) for n in range(2)]

    for t in range(0, slots, 2):
        for copy in left_copies[t] + left_copies[t + 1]:
            copy.wait()
        block = jnp.concatenate([jnp.concatenate(low(info[12 + t + n]), axis=1) for n in range(2)], axis=0)
        term = product(jnp.concatenate([left[t], left[t + 1]], axis=1), block)
        if t == 0:
            total[...] = term
        else:
            total[...] += term

    upper = right[2 * slots].reshape(width, width)
    one = total[:, :width]
    two = product(one, upper) - total[:, width:]
    keep[0] = -one[:width]
    give[0] = -one[width:]
    core = info[11]
    tiles = (second.shape[0], second.shape[2], width)
    second[:, core] = two[:width].reshape(tiles)
    second[:, 1 - core] = two[width:].reshape(tiles)
    away = info[8] > 0
    slot_one = jnp.where(away, -one[width:], -one[:width])
    slot_two = jnp.where(away, two[width:], two[:width])
    low_one, low_two = low(info[10])
    here = jnp.where(info[9] > 0, pivot[0], jnp.zeros_like(slot_one))
    diag = here - product(low_one, slot_one, 0, 0)
    cross = product(diag, upper) + product(slot_one, low_two, 0, 0)
    last = product(upper, cross, 0, 0) - product(low_two, slot_two, 0, 0)
    pieces, tall = parts.shape[0], parts.shape[1] // 3
    for n, term in enumerate((diag, cross, last)):
        parts[:, n * tall : (n + 1) * tall, :] = term.reshape(pieces, tall, width)


def level_blocks(info, arrivals, given, lows, pivot):
    width = pivot.shape[-1]
    slots = len(PLACES)
    pieces = slots
    cols = 2 * slots
    f32 = jnp.float32
    whole = lambda *shape: pl.BlockSpec(shape, lambda i, s: (0,) * len(shape))
    grid_spec = pltpu.PrefetchScalarGridSpec(
        num_scalar_prefetch=1,
        grid=(1,),
        in_specs=[pl.BlockSpec(memory_space=pl.ANY)] * (2 * len(ROUTE) + 3) + [whole(1, width, width)],
        out_specs=[
            whole(1, width, width),
            whole(1, width, width),
            whole(slots, 2, width // slots, width),
            whole(pieces, 3 * width // pieces, width),
        ],
        scratch_shapes=[
            pltpu.VMEM((2 * width, 2 * width), f32),
            pltpu.VMEM((slots, 2 * width, width), f32),
            pltpu.VMEM((2 * slots + 1, cols, width // cols, width), f32),
            pltpu.SemaphoreType.DMA((cols,)),
            pltpu.SemaphoreType.DMA((slots, 3)),
        ],
    )
    return pl.pallas_call(
        kernel,
        grid_spec=grid_spec,
        out_shape=[
            jax.ShapeDtypeStruct((1, width, width), f32),
            jax.ShapeDtypeStruct((1, width, width), f32),
            jax.ShapeDtypeStruct((slots, 2, width // slots, width), f32),
            jax.ShapeDtypeStruct((pieces, 3 * width // pieces, width), f32),
        ],
        compiler_params=pltpu.CompilerParams(vmem_limit_bytes=28 << 20),
        cost_estimate=pl.CostEstimate(flops=10_000_000_000, bytes_accessed=12_000_000, transcendentals=0),
    )(info, *arrivals, *given, *lows, pivot)


def exchange(x, axis):
    return lax.all_to_all(x, axis, split_axis=0, concat_axis=0, tiled=True)


def pick(x, index):
    return x.at[index].get(mode="promise_in_bounds")


def swap(x, axis=CORES):
    return lax.ppermute(x, axis, [(0, 1), (1, 0)])


def shift(x, axis, by):
    n = lax.axis_size(axis)
    return lax.ppermute(x, axis, [(i, (i + by) % n) for i in range(n)])


def go_round(*ways):
    hold = lax.optimization_barrier
    owns = hold([own for own, _, _ in ways])
    lines = [line for _, line, _ in ways]

    def both_ways(arrays):
        return [(shift(x, line, 1), shift(x, line, -1)) for x, line in zip(arrays, lines)]

    def onward(pairs):
        half = pairs[0][0].shape[0] // 2, pairs[1][0].shape[0] // 2
        return [
            (shift(low[:n], line, 1), shift(high[n:], line, -1))
            for (low, high), line, n in zip(pairs, lines, half)
        ]

    beside = [swap(own, neighbour) for own, (_, _, neighbour) in zip(owns, ways)]
    near = hold(both_ways(owns))
    across = onward(near)
    beside, across = hold((beside, across))
    far = hold(both_ways(beside))
    last = onward(far)
    return [(o, *n, *a, b, *f, *e) for o, n, a, b, f, e in zip(owns, near, across, beside, far, last)]


def body(anc, pattern, parents, low_one, pivot_one, low_two, factor, pivot_two):
    row, line, across, core = (lax.axis_index(a) for a in (ROWS, LINE, ACROSS, CORES))
    half = lax.axis_index(NEXT)
    rows, lines, pair, cores = (lax.axis_size(a) for a in (ROWS, LINE, ACROSS, CORES))
    chips = lines * pair
    cols = chips * cores
    width = pivot_one.shape[-1]
    piece = width // cols
    chip = line * pair + across
    col = chip * cores + core
    kind = jnp.arange(cols, dtype=jnp.int32)
    children = jnp.sum(jnp.where(parents[None, :] == kind[:, None], kind[None, :], 0), axis=1)

    flat = [x.reshape(cols, piece, width) for x in (low_one, low_two, factor)]
    pieces = exchange(jnp.concatenate(flat, axis=1), SIDE).reshape(3 * cols, piece, width)
    order = jnp.stack([3 * kind, 3 * children + 1], axis=1).reshape(-1)
    routed = pick(pieces, order).reshape(rows, cores * 2 * piece, width)
    own_children = lax.dynamic_slice_in_dim(children, row * cores, cores)
    uppers = pick(pieces, 3 * own_children + 2)
    upper = swap(lax.dynamic_index_in_dim(uppers, 1 - core, 0))
    kept = lax.dynamic_index_in_dim(uppers, core, 0)
    uppers = jnp.where(core == 0, jnp.stack([kept, upper]), jnp.stack([upper, kept]))
    mine = exchange(routed.reshape(cols, 2 * piece, width), (*ROWS, CORES))
    mine = mine.reshape(rows, cores, 2, piece, width).transpose(1, 0, 2, 3, 4)
    both = jnp.concatenate([mine.reshape(cores, rows * 2, piece, width), uppers], axis=1)

    ring = lax.axis_index(RING)
    lengths = lax.axis_size(RING)
    slot = jnp.stack([(half ^ n) * lengths + (ring + m) % lengths for m, n in PLACES])
    places = jnp.stack([(line + m) % lines * pair + (across ^ n) for m, n in PLACES])
    here = pick(pattern, row * cores + core)
    picks = pick(pick(pattern, row * cores + 1 - core), slot) % 2 > 0
    away = pick(here, chip) != col
    flags = jnp.stack([away.astype(jnp.int32), (chip == row).astype(jnp.int32), chip, core])
    info = jnp.concatenate([pick(here, slot) % 2, flags, slot, places])
    info, picks, anc, both = lax.optimization_barrier((info, picks, anc, both))

    inverse, lows = go_round((anc, RING, NEXT), (both, LINE, ACROSS))

    def handed(first, *blocks):
        picked = [jnp.where(picks[first + n], x[:, width:], x[:, :width]) for n, x in enumerate(blocks)]
        return swap(jnp.stack(picked))

    own, below, above, low_across, high_across, beside, up, down, low_far, high_far = inverse
    given = (
        handed(0, own, below, above, jnp.concatenate([low_across, high_across]), beside),
        handed(5, up, down),
        handed(7, jnp.concatenate([low_far, high_far])),
    )
    keep, give, second, parts = level_blocks(info, inverse, given, lows, pivot_one)
    taken = swap(give)
    column_one = jnp.where(core == 0, jnp.concatenate([keep, taken]), jnp.concatenate([taken, keep]))

    summed = jnp.sum(exchange(parts, CHIPS), axis=0)
    halves = summed.reshape(3, cores, piece, width).transpose(1, 0, 2, 3).reshape(1, cores, 3 * piece, width)
    halves = jnp.broadcast_to(halves, (rows, *halves.shape[1:]))
    send = jnp.concatenate([halves, second], axis=2).reshape(cols, -1, width)
    known = exchange(send, (*ROWS, CORES))
    column_two = pick(known[:, 3 * piece :], parents)
    column_two = exchange(column_two.reshape(rows, -1, width), ROWS)
    column_two = column_two.reshape(rows, cores, -1, width).transpose(1, 0, 2, 3)
    known = known.reshape(cols, -1, piece, width)
    blocks = [known[:, 0], pick(known[:, 1:3], parents).reshape(cols, -1, width)]
    final = exchange(jnp.concatenate(blocks, axis=1), SIDE)
    final = final.reshape(cols, 3, piece, width)
    diag_one, cross, last = (final[:, n].reshape(1, width, width) for n in range(3))
    return column_one, diag_one, column_two.reshape(cores, width, width), -cross, pivot_two + last


def solution(mesh):
    rows, cols = mesh.devices.shape
    cut = Mesh(mesh.devices.reshape(2, rows // 2, cols // 4, 2, 2), (*ROWS, *SIDE))
    flat, wide = P(SIDE, None, None), P(SIDE, ROWS, None)
    return jax.shard_map(
        body,
        mesh=cut,
        in_specs=(P(SIDE, ROWS), P(), P(), wide, flat, wide, flat, flat),
        out_specs=(P(ROWS, SIDE, None), flat, P(ROWS, SIDE, None), flat, flat),
        check_vma=False,
    )
```

```python
import functools

import jax
import jax.numpy as jnp
from jax import lax
from jax.experimental import pallas as pl
from jax.experimental.pallas import tpu as pltpu
from jax.sharding import Mesh, PartitionSpec as P

NEXT, RING, LINE, ACROSS, CORES = "next", "ring", "x", "across", "core"
ROWS = (NEXT, RING)
CHIPS = (LINE, ACROSS)
SIDE = (*CHIPS, CORES)


def split(x):
    high = x.astype(jnp.bfloat16)
    return high, (x - high.astype(jnp.float32)).astype(jnp.bfloat16)


def product(a, b, a_dim=1, b_dim=0):
    (ah, al), (bh, bl) = split(a), split(b)
    left = jnp.concatenate([ah, ah, al], axis=a_dim)
    right = jnp.concatenate([bh, bl, bh], axis=b_dim)
    dims = (((a_dim,), (b_dim,)), ((), ()))
    return lax.dot_general(left, right, dims, preferred_element_type=jnp.float32)


ROUTE = (
    ((0, 0, 0), (0, 0, 1)),
    ((-1, 0, 0), (-1, 0, 1)),
    ((1, 0, 0), (1, 0, 1)),
    ((2, 0, 0),),
    ((2, 0, 1),),
    ((0, 1, 0), (0, 1, 1)),
    ((-1, 1, 0), (-1, 1, 1)),
    ((1, 1, 0), (1, 1, 1)),
    ((2, 1, 0),),
    ((2, 1, 1),),
)
PLACES = ((0, 0), (-1, 0), (1, 0), (2, 0), (0, 1), (-1, 1), (1, 1), (2, 1))
GROUPS = (0, 5, 7)


def kernel(info, *refs):
    arrivals, refs = refs[: len(ROUTE)], refs[len(ROUTE) :]
    given, refs = refs[:3], refs[3:]
    lows, refs = refs[: len(ROUTE)], refs[len(ROUTE) :]
    pivot, keep, give, second, parts, total, left, right, low_done, left_done = refs
    slots, width = left.shape[0], left.shape[-1]

    low_copies = []
    for ref, entries in zip(lows, ROUTE):
        for n, (along, beside, part) in enumerate(entries):
            col = 2 * info[20 + PLACES.index((along, beside))] + part
            done = low_done.at[len(low_copies)]
            low_copies.append(pltpu.make_async_copy(ref.at[n], right.at[:, col], done))
    left_copies = [[] for _ in range(slots)]
    parts_of = width // 2
    for which, (ref, entries) in enumerate(zip(arrivals, ROUTE)):
        for n, (along, beside, part) in enumerate(entries):
            t = PLACES.index((along, beside))
            half = pl.ds(pl.multiple_of(info[t] * width, width), width)
            source = ref.at[pl.ds(n * parts_of, parts_of), half]
            target = left.at[t, pl.ds(part * parts_of, parts_of)]
            left_copies[t].append(pltpu.make_async_copy(source, target, left_done.at[t, part]))
    for t in range(slots):
        group = sum(t >= first for first in GROUPS) - 1
        source = given[group].at[t - GROUPS[group]]
        left_copies[t].append(pltpu.make_async_copy(source, left.at[t, pl.ds(width, width)], left_done.at[t, 2]))
    for copy in low_copies:
        copy.start()
    for copies in left_copies:
        for copy in copies:
            copy.start()
    for copy in low_copies:
        copy.wait()

    def low(row):
        return [right[2 * row + n].reshape(width, width) for n in range(2)]

    for t in range(0, slots, 2):
        for copy in left_copies[t] + left_copies[t + 1]:
            copy.wait()
        block = jnp.concatenate([jnp.concatenate(low(info[12 + t + n]), axis=1) for n in range(2)], axis=0)
        term = product(jnp.concatenate([left[t], left[t + 1]], axis=1), block)
        if t == 0:
            total[...] = term
        else:
            total[...] += term

    upper = right[2 * slots].reshape(width, width)
    one = total[:, :width]
    two = product(one, upper) - total[:, width:]
    keep[0] = -one[:width]
    give[0] = -one[width:]
    core = info[11]
    tiles = (second.shape[0], second.shape[2], width)
    second[:, core] = two[:width].reshape(tiles)
    second[:, 1 - core] = two[width:].reshape(tiles)
    away = info[8] > 0
    slot_one = jnp.where(away, -one[width:], -one[:width])
    slot_two = jnp.where(away, two[width:], two[:width])
    low_one, low_two = low(info[10])
    here = jnp.where(info[9] > 0, pivot[0], jnp.zeros_like(slot_one))
    diag = here - product(low_one, slot_one, 0, 0)
    cross = product(diag, upper) + product(slot_one, low_two, 0, 0)
    last = product(upper, cross, 0, 0) - product(low_two, slot_two, 0, 0)
    pieces, tall = parts.shape[0], parts.shape[1] // 3
    for n, term in enumerate((diag, cross, last)):
        parts[:, n * tall : (n + 1) * tall, :] = term.reshape(pieces, tall, width)


def level_blocks(info, arrivals, given, lows, pivot):
    width = pivot.shape[-1]
    slots = len(PLACES)
    pieces = slots
    cols = 2 * slots
    f32 = jnp.float32
    whole = lambda *shape: pl.BlockSpec(shape, lambda i, s: (0,) * len(shape))
    grid_spec = pltpu.PrefetchScalarGridSpec(
        num_scalar_prefetch=1,
        grid=(1,),
        in_specs=[pl.BlockSpec(memory_space=pl.ANY)] * (2 * len(ROUTE) + 3) + [whole(1, width, width)],
        out_specs=[
            whole(1, width, width),
            whole(1, width, width),
            whole(slots, 2, width // slots, width),
            whole(pieces, 3 * width // pieces, width),
        ],
        scratch_shapes=[
            pltpu.VMEM((2 * width, 2 * width), f32),
            pltpu.VMEM((slots, 2 * width, width), f32),
            pltpu.VMEM((2 * slots + 1, cols, width // cols, width), f32),
            pltpu.SemaphoreType.DMA((cols,)),
            pltpu.SemaphoreType.DMA((slots, 3)),
        ],
    )
    return pl.pallas_call(
        kernel,
        grid_spec=grid_spec,
        out_shape=[
            jax.ShapeDtypeStruct((1, width, width), f32),
            jax.ShapeDtypeStruct((1, width, width), f32),
            jax.ShapeDtypeStruct((slots, 2, width // slots, width), f32),
            jax.ShapeDtypeStruct((pieces, 3 * width // pieces, width), f32),
        ],
        compiler_params=pltpu.CompilerParams(vmem_limit_bytes=28 << 20),
        cost_estimate=pl.CostEstimate(flops=10_000_000_000, bytes_accessed=12_000_000, transcendentals=0),
    )(info, *arrivals, *given, *lows, pivot)


def exchange(x, axis):
    return lax.all_to_all(x, axis, split_axis=0, concat_axis=0, tiled=True)


def pick(x, index):
    return x.at[index].get(mode="promise_in_bounds")


def swap(x, axis=CORES):
    return lax.ppermute(x, axis, [(0, 1), (1, 0)])


def shift(x, axis, by):
    n = lax.axis_size(axis)
    return lax.ppermute(x, axis, [(i, (i + by) % n) for i in range(n)])


def go_round(*ways):
    hold = lax.optimization_barrier
    first = swap(ways[0][0], ways[0][2])
    owns, first = hold(([own for own, _, _ in ways], first))
    lines = [line for _, line, _ in ways]

    def both_ways(arrays):
        return [(shift(x, line, 1), shift(x, line, -1)) for x, line in zip(arrays, lines)]

    def onward(pairs):
        half = pairs[0][0].shape[0] // 2, pairs[1][0].shape[0] // 2
        return [
            (shift(low[:n], line, 1), shift(high[n:], line, -1))
            for (low, high), line, n in zip(pairs, lines, half)
        ]

    beside = [first, swap(owns[1], ways[1][2])]
    near = hold(both_ways(owns))
    across = onward(near)
    beside, across = hold((beside, across))
    far = hold(both_ways(beside))
    last = onward(far)
    return [(o, *n, *a, b, *f, *e) for o, n, a, b, f, e in zip(owns, near, across, beside, far, last)]


def body(anc, pattern, parents, low_one, pivot_one, low_two, factor, pivot_two):
    row, line, across, core = (lax.axis_index(a) for a in (ROWS, LINE, ACROSS, CORES))
    half = lax.axis_index(NEXT)
    rows, lines, pair, cores = (lax.axis_size(a) for a in (ROWS, LINE, ACROSS, CORES))
    chips = lines * pair
    cols = chips * cores
    width = pivot_one.shape[-1]
    piece = width // cols
    chip = line * pair + across
    col = chip * cores + core
    kind = jnp.arange(cols, dtype=jnp.int32)
    children = jnp.sum(jnp.where(parents[None, :] == kind[:, None], kind[None, :], 0), axis=1)

    flat = [x.reshape(cols, piece, width) for x in (low_one, low_two, factor)]
    pieces = exchange(jnp.concatenate(flat, axis=1), SIDE).reshape(3 * cols, piece, width)
    order = jnp.stack([3 * kind, 3 * children + 1], axis=1).reshape(-1)
    routed = pick(pieces, order).reshape(rows, cores * 2 * piece, width)
    own_children = lax.dynamic_slice_in_dim(children, row * cores, cores)
    uppers = pick(pieces, 3 * own_children + 2)
    upper = swap(lax.dynamic_index_in_dim(uppers, 1 - core, 0))
    kept = lax.dynamic_index_in_dim(uppers, core, 0)
    uppers = jnp.where(core == 0, jnp.stack([kept, upper]), jnp.stack([upper, kept]))
    mine = exchange(routed.reshape(cols, 2 * piece, width), (*ROWS, CORES))
    mine = mine.reshape(rows, cores, 2, piece, width).transpose(1, 0, 2, 3, 4)
    both = jnp.concatenate([mine.reshape(cores, rows * 2, piece, width), uppers], axis=1)

    ring = lax.axis_index(RING)
    lengths = lax.axis_size(RING)
    slot = jnp.stack([(half ^ n) * lengths + (ring + m) % lengths for m, n in PLACES])
    places = jnp.stack([(line + m) % lines * pair + (across ^ n) for m, n in PLACES])
    here = pick(pattern, row * cores + core)
    picks = pick(pick(pattern, row * cores + 1 - core), slot) % 2 > 0
    away = pick(here, chip) != col
    flags = jnp.stack([away.astype(jnp.int32), (chip == row).astype(jnp.int32), chip, core])
    info = jnp.concatenate([pick(here, slot) % 2, flags, slot, places])
    info, picks, both = lax.optimization_barrier((info, picks, both))

    inverse, lows = go_round((anc, RING, NEXT), (both, LINE, ACROSS))

    def handed(first, *blocks):
        picked = [jnp.where(picks[first + n], x[:, width:], x[:, :width]) for n, x in enumerate(blocks)]
        return swap(jnp.stack(picked))

    own, below, above, low_across, high_across, beside, up, down, low_far, high_far = inverse
    given = (
        handed(0, own, below, above, jnp.concatenate([low_across, high_across]), beside),
        handed(5, up, down),
        handed(7, jnp.concatenate([low_far, high_far])),
    )
    keep, give, second, parts = level_blocks(info, inverse, given, lows, pivot_one)
    taken = swap(give)
    column_one = jnp.where(core == 0, jnp.concatenate([keep, taken]), jnp.concatenate([taken, keep]))

    summed = jnp.sum(exchange(parts, CHIPS), axis=0)
    halves = summed.reshape(3, cores, piece, width).transpose(1, 0, 2, 3).reshape(1, cores, 3 * piece, width)
    halves = jnp.broadcast_to(halves, (rows, *halves.shape[1:]))
    send = jnp.concatenate([halves, second], axis=2).reshape(cols, -1, width)
    known = exchange(send, (*ROWS, CORES))
    column_two = pick(known[:, 3 * piece :], parents)
    column_two = exchange(column_two.reshape(rows, -1, width), ROWS)
    column_two = column_two.reshape(rows, cores, -1, width).transpose(1, 0, 2, 3)
    known = known.reshape(cols, -1, piece, width)
    blocks = [known[:, 0], pick(known[:, 1:3], parents).reshape(cols, -1, width)]
    final = exchange(jnp.concatenate(blocks, axis=1), SIDE)
    final = final.reshape(cols, 3, piece, width)
    diag_one, cross, last = (final[:, n].reshape(1, width, width) for n in range(3))
    return column_one, diag_one, column_two.reshape(cores, width, width), -cross, pivot_two + last


def solution(mesh):
    rows, cols = mesh.devices.shape
    cut = Mesh(mesh.devices.reshape(2, rows // 2, cols // 4, 2, 2), (*ROWS, *SIDE))
    flat, wide = P(SIDE, None, None), P(SIDE, ROWS, None)
    return jax.shard_map(
        body,
        mesh=cut,
        in_specs=(P(SIDE, ROWS), P(), P(), wide, flat, wide, flat, flat),
        out_specs=(P(ROWS, SIDE, None), flat, P(ROWS, SIDE, None), flat, flat),
        check_vma=False,
    )
```
